256 devices in a mesh: wide: 16 (over y, z_hi), narrow: 16 (over x, z_lo, core).
Axes of the slice: x: 4, y: 4, z: 8 (z_hi: 4, z_lo: 2; z = z_hi * 2 + z_lo), core: 2. Of those that a mesh axis runs over, the one named last changes fastest.
Arguments:
- features: bfloat16 [65536, 768], P(('wide', 'narrow'))
- proj_weight: bfloat16 [768, 512], replicated, may hold values from -0.21875 to 0.21875
- bias: float32 [512], replicated, may hold values from -1.5 to 1.5
- disc_weight: float32 [512, 512], replicated, may hold values from -0.25 to 0.25
- adjacency: int32 [16, 16, 24, 256, 256], P('wide', 'narrow'), may hold values from 0 to 3
- row_block: int32 [16, 16, 24], P('wide', 'narrow'), may hold values from 0 to 15
- col_block: int32 [16, 16, 24], P('wide', 'narrow'), may hold values from 0 to 15
- block_count: int32 [16, 16], P('wide', 'narrow'), may hold values from 1 to 24, as said below
- degree: int32 [65536], replicated, may hold values from 6 to 65
- corrupt_source: int32 [256], replicated, may hold values from 0 to 255, as said below
Outputs:
- hidden: bfloat16 [65536, 512], P(('wide', 'narrow'))
- scores: float32 [2, 65536], P(None, ('wide', 'narrow'))
- loss: float32 [], replicated
The draws below stay inside these ranges and needn't reach their ends.
Inputs may be any that keep to these rules, and one draw needn't show every extreme that they name: Only slots below block_count of a tile take part; some tile holds 24 live slots in every draw. corrupt_source is a permutation of the blocks, and block g and block corrupt_source[g] have equal g % 16.
All inputs are finite; a program needn't handle non-finite values.
Results may differ from the reference program's by a relative error of at most 0.0056.
Values may be sent and summed in bfloat16 or wider, within the bound.
No kernel may reach another device: no remote copies, remote signals or barrier semaphores. Data moves between devices by JAX's collectives and lax.ppermute only.
A program may use at most 128 MiB of HBM per device.

```python
import jax
import jax.numpy as jnp
from jax import lax

F = 768
HID = 512
BLK = 256
NB = 24
ROWS_DEV = 256
NODES = 65536
NBLOCKS = 256
RB = 1
TR = 16
TC = 16
N_WIDE = 16
N_NARROW = 16


def draw_features(key, part):
    position = jnp.arange(NODES, dtype=jnp.float32)[:, None] / NODES
    values = jax.random.normal(key, (NODES, F), jnp.float32)
    values = values * (1.0 + 2.0 * position)
    return values.astype(jnp.bfloat16)


def draw_adjacency(key, part):
    values = jax.random.randint(key, (N_WIDE, N_NARROW, NB, BLK, BLK), 0, 30)
    return jnp.maximum(values - 26, 0).astype(jnp.int32)


def draw_block_count(key, part):
    shifts = jax.random.randint(key, (N_WIDE * N_NARROW,), 0, 4)
    counts = jnp.maximum(NB // jnp.power(2, shifts), 1)
    chosen = jax.random.randint(jax.random.fold_in(key, 7), (), 0, N_WIDE * N_NARROW)
    counts = jnp.where(jnp.arange(N_WIDE * N_NARROW) == chosen, NB, counts)
    return counts.reshape(N_WIDE, N_NARROW).astype(jnp.int32)


def draw_degree(key, part):
    position = jnp.arange(NODES, dtype=jnp.int32)
    upper = 7 + 59 * (NODES - position) // NODES
    return jax.random.randint(key, (NODES,), 6, upper).astype(jnp.int32)


def draw_corrupt_source(key, part):
    blocks = jnp.arange(NBLOCKS, dtype=jnp.int32)
    group = blocks // RB % N_NARROW
    scale = 4096 * NBLOCKS
    shuffle = jax.random.randint(key, (NBLOCKS,), 0, 4096) * NBLOCKS + blocks
    shuffled = jnp.argsort(group * scale + shuffle, stable=True)
    ordered = jnp.argsort(group * scale + blocks, stable=True)
    source = jnp.zeros((NBLOCKS,), jnp.int32).at[ordered].set(shuffled.astype(jnp.int32))
    return source


def plant(values, rng, least, top_value):
    spot = [jax.random.randint(jax.random.fold_in(rng, axis), (), 0, length) for axis, length in enumerate(values.shape)]
    main_axis = values.shape.index(max(values.shape))
    next_to = spot[:main_axis] + [(spot[main_axis] + 1) % values.shape[main_axis]] + spot[main_axis + 1:]
    return values.at[tuple(spot)].set(least).at[tuple(next_to)].set(top_value)


def gaussian(own_key, dims, deviation, limit, held_as=jnp.bfloat16):
    array = jax.random.normal(own_key, dims, jnp.float32) * deviation
    return jnp.minimum(jnp.maximum(array, -limit), limit).astype(held_as)


def setup_inputs(seed: int = 0) -> dict:
    splits = jax.random.split(jax.random.key(seed), 11)
    features = draw_features(jax.random.fold_in(splits[10], 71), 0)
    proj_weight = gaussian(splits[1], (F, HID), F ** -0.5, 0.21875)
    bias = gaussian(splits[2], (HID,), 0.3, 1.5, jnp.float32)
    disc_weight = gaussian(splits[3], (HID, HID), HID ** -0.5, 0.25, jnp.float32)
    adjacency = draw_adjacency(jax.random.fold_in(splits[10], 71), 0)
    row_block = plant(jax.random.randint(splits[5], (N_WIDE, N_NARROW, NB), 0, TR), jax.random.fold_in(splits[5], 1), 0, TR - 1).astype(jnp.int32)
    col_block = plant(jax.random.randint(splits[6], (N_WIDE, N_NARROW, NB), 0, TC), jax.random.fold_in(splits[6], 1), 0, TC - 1).astype(jnp.int32)
    block_count = draw_block_count(jax.random.fold_in(splits[10], 71), 0)
    degree = draw_degree(jax.random.fold_in(splits[10], 71), 0)
    corrupt_source = draw_corrupt_source(jax.random.fold_in(splits[10], 71), 0)
    return {"features": features, "proj_weight": proj_weight, "bias": bias, "disc_weight": disc_weight, "adjacency": adjacency, "row_block": row_block, "col_block": col_block, "block_count": block_count, "degree": degree, "corrupt_source": corrupt_source}


def reference(features, proj_weight, bias, disc_weight, adjacency, row_block, col_block, block_count, degree, corrupt_source):
    projected = jnp.dot(features, proj_weight, preferred_element_type=jnp.float32).astype(jnp.bfloat16)
    corrupted = projected.reshape(NBLOCKS, BLK, HID)[corrupt_source].reshape(NODES, HID)
    inv_root = lax.rsqrt(degree.astype(jnp.float32))
    clean_cols = projected.reshape(N_WIDE, N_NARROW, ROWS_DEV, HID)
    corrupt_cols = corrupted.reshape(N_WIDE, N_NARROW, ROWS_DEV, HID)
    root_cols = inv_root.reshape(N_WIDE, N_NARROW, ROWS_DEV)
    root_rows = inv_root.reshape(N_WIDE, TR, BLK)

    def tile_step(tile, totals):
        wide_at = (tile // N_NARROW).astype(jnp.int32)
        narrow_at = (tile % N_NARROW).astype(jnp.int32)
        clean_panel = clean_cols[:, narrow_at].reshape(TC, BLK, HID)
        corrupt_panel = corrupt_cols[:, narrow_at].reshape(TC, BLK, HID)
        both_panel = jnp.concatenate((clean_panel, corrupt_panel), axis=2)
        col_roots = root_cols[:, narrow_at].reshape(TC, BLK)
        row_roots = root_rows[wide_at]
        tile_adjacency = adjacency[wide_at, narrow_at]
        tile_rows = row_block[wide_at, narrow_at]
        tile_cols = col_block[wide_at, narrow_at]

        def slot_step(slot, accum):
            row_at = tile_rows[slot]
            col_at = tile_cols[slot]
            normed = (tile_adjacency[slot].astype(jnp.float32) * row_roots[row_at][:, None] * col_roots[col_at][None, :]).astype(jnp.bfloat16)
            term = jnp.dot(normed, both_panel[col_at], preferred_element_type=jnp.float32)
            return accum.at[row_at].add(term)
        accum = lax.fori_loop(jnp.int32(0), block_count[wide_at, narrow_at], slot_step, jnp.zeros((TR, BLK, 2 * HID), jnp.float32))
        return totals.at[wide_at].add(accum)
    totals = lax.fori_loop(0, N_WIDE * N_NARROW, tile_step, jnp.zeros((N_WIDE, TR, BLK, 2 * HID), jnp.float32))
    summed = totals.reshape(NODES, 2 * HID)
    degree_float = degree.astype(jnp.float32)[:, None]
    clean_h = jnp.maximum(summed[:, :HID] + projected.astype(jnp.float32) / degree_float + bias, 0.0)
    corrupt_h = jnp.maximum(summed[:, HID:] + corrupted.astype(jnp.float32) / degree_float + bias, 0.0)
    summary = jax.nn.sigmoid(lax.optimization_barrier(jnp.sum(clean_h, axis=0)) / NODES)
    probe = jnp.dot(disc_weight, summary, precision=lax.Precision.HIGHEST)
    clean_score = jnp.dot(clean_h, probe, precision=lax.Precision.HIGHEST)
    corrupt_score = jnp.dot(corrupt_h, probe, precision=lax.Precision.HIGHEST)
    loss = (jnp.sum(jax.nn.softplus(-clean_score)) + jnp.sum(jax.nn.softplus(corrupt_score))) / (2 * NODES)
    return (clean_h.astype(jnp.bfloat16), jnp.stack((clean_score, corrupt_score)), loss)
```

```python
import functools

import jax
import jax.numpy as jnp
from jax import lax
from jax.experimental import pallas as pl
from jax.experimental.pallas import tpu as pltpu
from jax.sharding import PartitionSpec as P


X, ZL, CORES = 4, 2, 2
Y, ZH = 4, 4
BOTH = ("wide", "narrow")


def narrow_perm(dx=0, flip_z=0, flip_core=0):
    pairs = []
    for x in range(X):
        for zl in range(ZL):
            for core in range(CORES):
                target = (((x + dx) % X) * ZL + (zl ^ flip_z)) * CORES + (core ^ flip_core)
                pairs.append(((x * ZL + zl) * CORES + core, target))
    return pairs


def wide_perm(dy=0, dz=0):
    return [
        (y * ZH + zh, ((y + dy) % Y) * ZH + (zh + dz) % ZH) for y in range(Y) for zh in range(ZH)
    ]


def to_narrow(value, **steps):
    return lax.ppermute(value, "narrow", narrow_perm(**steps))


def to_wide(value, **steps):
    return lax.ppermute(value, "wide", wide_perm(**steps))


SLOTS = 24
ORDER, COL, SRC, START, ROWS, DEST, OWN = 0, 24, 48, 72, 89, 97, 113
META = 128


def spmm_kernel(split, meta, normed, *refs):
    pieces, (out, own), (panel, acc, sem) = refs[:8], refs[8:10], refs[10:]
    step = pl.program_id(0)
    half = panel.shape[2]

    @pl.when(step == 0)
    def _():
        copies = []
        for k in range(Y):
            for j in range(ZH):
                c = meta[DEST + k * ZH + j]
                copies.append(
                    pltpu.make_async_copy(
                        pieces[k].at[j], panel.at[c, pl.ds(0, split)], sem.at[len(copies)]
                    )
                )
                copies.append(
                    pltpu.make_async_copy(
                        pieces[Y + j].at[k],
                        panel.at[c, pl.ds(split, panel.shape[1] - split)],
                        sem.at[len(copies)],
                    )
                )
        for copy in copies:
            copy.start()
        for copy in copies:
            copy.wait()
        own[...] = panel[meta[OWN]]

    row = meta[ROWS + step]
    acc[...] = jnp.zeros_like(acc)

    def add_slot(at, carry):
        slot = meta[ORDER + at]
        block = normed[slot]
        acc[:, :half] += jnp.dot(block, panel[meta[COL + slot]], preferred_element_type=jnp.float32)
        acc[:, half:] += jnp.dot(block, panel[meta[SRC + slot]], preferred_element_type=jnp.float32)
        return carry

    lax.fori_loop(meta[START + row], meta[START + row + 1], add_slot, 0)
    out[0] = acc[...].astype(out.dtype)


def spmm(split, rows, block_len, hidden, meta, normed, pieces):
    slots = normed.shape[0]
    return pl.pallas_call(
        functools.partial(spmm_kernel, split),
        grid=(rows,),
        in_specs=[
            pl.BlockSpec(memory_space=pltpu.SMEM),
            pl.BlockSpec((slots, block_len, block_len), lambda i: (0, 0, 0)),
        ]
        + [pl.BlockSpec(memory_space=pl.ANY)] * len(pieces),
        out_specs=[
            pl.BlockSpec((1, block_len, 2 * hidden), lambda i: (i, 0, 0)),
            pl.BlockSpec((block_len, hidden), lambda i: (0, 0)),
        ],
        out_shape=[
            jax.ShapeDtypeStruct((rows, block_len, 2 * hidden), jnp.bfloat16),
            jax.ShapeDtypeStruct((block_len, hidden), jnp.bfloat16),
        ],
        scratch_shapes=[
            pltpu.VMEM((Y * ZH, block_len, hidden), jnp.bfloat16),
            pltpu.VMEM((block_len, 2 * hidden), jnp.float32),
            pltpu.SemaphoreType.DMA((2 * Y * ZH,)),
        ],
        compiler_params=pltpu.CompilerParams(vmem_limit_bytes=40 * 1024 * 1024),
        cost_estimate=pl.CostEstimate(
            flops=slots * block_len * block_len * 2 * hidden,
            bytes_accessed=14 * 1024 * 1024,
            transcendentals=0,
        ),
    )(meta, normed, *pieces)


def total_over_devices(value, devices):
    spread = jnp.broadcast_to(value, (devices,) + value.shape)
    gathered = lax.all_to_all(spread, BOTH, 0, 0)
    return jnp.sum(gathered.astype(jnp.float32), axis=0)


def shards(
    features,
    proj_weight,
    bias,
    disc_weight,
    adjacency,
    row_block,
    col_block,
    block_count,
    degree,
    corrupt_source,
):
    block_len = adjacency.shape[-1]
    hidden = proj_weight.shape[1]
    wide_size = lax.axis_size("wide")
    narrow_size = lax.axis_size("narrow")
    devices = wide_size * narrow_size
    wide_at = lax.axis_index("wide")
    narrow_at = lax.axis_index("narrow")
    y, zh = wide_at // ZH, wide_at % ZH
    x, zl, core = narrow_at // (ZL * CORES), narrow_at // CORES % ZL, narrow_at % CORES

    own = jnp.dot(features, proj_weight, preferred_element_type=jnp.float32).astype(jnp.bfloat16)

    split = 176
    first, second = own[:split], own[split:]
    by_z = [first] + [to_wide(first, dz=k) for k in range(1, ZH)]
    by_y = [second] + [to_wide(second, dy=k) for k in range(1, Y)]
    by_z = jnp.stack(by_z)
    by_y = jnp.stack(by_y)
    pieces = [by_z] + [to_wide(by_z, dy=k) for k in range(1, Y)]
    pieces += [by_y] + [to_wide(by_y, dz=k) for k in range(1, ZH)]

    inv_root = lax.rsqrt(degree.astype(jnp.float32))
    col_roots = lax.dynamic_index_in_dim(
        inv_root.reshape(wide_size, narrow_size, block_len), narrow_at, 1, keepdims=False
    )
    row_roots = lax.dynamic_index_in_dim(
        inv_root.reshape(wide_size, narrow_size, block_len), wide_at, 0, keepdims=False
    )
    slot_rows = row_block[0, 0]
    slot_cols = col_block[0, 0]
    normed = (
        adjacency[0, 0].astype(jnp.float32)
        * row_roots[slot_rows][:, :, None]
        * col_roots[slot_cols][:, None, :]
    ).astype(jnp.bfloat16)

    slot_ids = jnp.arange(SLOTS, dtype=jnp.int32)
    keys = jnp.where(slot_ids < block_count[0, 0], slot_rows, narrow_size)
    before = (keys[None, :] < keys[:, None]) | (
        (keys[None, :] == keys[:, None]) & (slot_ids[None, :] < slot_ids[:, None])
    )
    rank = jnp.sum(before.astype(jnp.int32), axis=1)
    order = jnp.sum(jnp.where(rank[None, :] == slot_ids[:, None], slot_ids[None, :], 0), axis=1)
    starts = jnp.sum(
        (keys[None, :] < jnp.arange(narrow_size + 1, dtype=jnp.int32)[:, None]).astype(jnp.int32),
        axis=1,
    )
    columns = jnp.arange(wide_size, dtype=jnp.int32)
    sources = (
        lax.dynamic_index_in_dim(
            corrupt_source.reshape(wide_size, narrow_size), narrow_at, 1, keepdims=False
        )
        // narrow_size
    )
    slot_sources = jnp.sum(
        jnp.where(slot_cols[:, None] == columns[None, :], sources[None, :], 0), axis=1
    )
    own_source = jnp.sum(jnp.where(columns == wide_at, sources, 0))
    steps_x = jnp.arange(X, dtype=jnp.int32)
    flips = jnp.arange(ZL, dtype=jnp.int32)
    targets = ((x + steps_x)[None, :] % X * ZL + (zl ^ flips)[:, None]) * CORES
    dest = (y - jnp.arange(Y, dtype=jnp.int32))[:, None] % Y * ZH + (
        zh - jnp.arange(ZH, dtype=jnp.int32)
    )[None, :] % ZH

    def tables(parity):
        parts = [
            order,
            slot_cols,
            slot_sources,
            starts,
            (targets + parity).reshape(-1),
            dest.reshape(-1),
            own_source[None],
        ]
        parts.append(jnp.zeros((META - sum(part.shape[0] for part in parts),), jnp.int32))
        return jnp.concatenate([part.astype(jnp.int32) for part in parts])

    rows = X * ZL
    sent, _ = spmm(split, rows, block_len, hidden, tables(1 - core), normed, pieces)
    kept, own_corrupt = spmm(split, rows, block_len, hidden, tables(core), normed, pieces)
    arrived = to_narrow(sent, flip_core=1)

    kept = kept.reshape(ZL, X, block_len, 2 * hidden)
    arrived = arrived.reshape(ZL, X, block_len, 2 * hidden)

    def joined(z_range, x_range, columns_from):
        at = (z_range, x_range, slice(None), slice(columns_from, columns_from + hidden))
        return (kept[at].astype(jnp.float32) + arrived[at].astype(jnp.float32)).astype(jnp.bfloat16)

    clean_far = joined(1, slice(None), 0)
    clean_near = joined(0, slice(None), 0)
    corrupt_parts = [joined(slice(None), k, hidden) for k in range(X)]
    clean_got = to_narrow(clean_far, flip_z=1)
    corrupt_got = [to_narrow(corrupt_parts[k], dx=k) for k in range(1, X)]
    clean_near = clean_near.astype(jnp.float32) + clean_got.astype(jnp.float32)
    clean_parts = clean_near.astype(jnp.bfloat16)
    corrupt_near = corrupt_parts[0].astype(jnp.float32) + sum(
        got.astype(jnp.float32) for got in corrupt_got
    )
    corrupt_far = corrupt_near[1].astype(jnp.bfloat16)
    clean_last = [to_narrow(clean_parts[k], dx=k) for k in range(1, X)]
    corrupt_last = to_narrow(corrupt_far, flip_z=1)
    clean_sum = clean_near[0] + sum(got.astype(jnp.float32) for got in clean_last)
    corrupt_sum = corrupt_near[0] + corrupt_last.astype(jnp.float32)

    own_degree = lax.dynamic_index_in_dim(
        degree.reshape(devices, block_len), wide_at * narrow_size + narrow_at, 0, keepdims=False
    )
    degree_float = own_degree.astype(jnp.float32)[:, None]
    clean_h = jnp.maximum(clean_sum + own.astype(jnp.float32) / degree_float + bias, 0.0)
    corrupt_h = jnp.maximum(
        corrupt_sum + own_corrupt.astype(jnp.float32) / degree_float + bias, 0.0
    )
    nodes = block_len * devices
    column_total = total_over_devices(jnp.sum(clean_h, axis=0), devices)
    summary = jax.nn.sigmoid(column_total / nodes)
    probe = jnp.dot(disc_weight, summary, precision=lax.Precision.HIGHEST)
    clean_score = jnp.dot(clean_h, probe, precision=lax.Precision.HIGHEST)
    corrupt_score = jnp.dot(corrupt_h, probe, precision=lax.Precision.HIGHEST)
    local_terms = jnp.sum(jax.nn.softplus(-clean_score)) + jnp.sum(jax.nn.softplus(corrupt_score))
    loss = total_over_devices(jnp.broadcast_to(local_terms, (128,)), devices)[0] / (2 * nodes)
    return (clean_h.astype(jnp.bfloat16), jnp.stack((clean_score, corrupt_score)), loss)


def solution(mesh):
    placed = (
        P(("wide", "narrow"), None),
        P(),
        P(),
        P(),
        P("wide", "narrow", None, None, None),
        P("wide", "narrow", None),
        P("wide", "narrow", None),
        P("wide", "narrow"),
        P(),
        P(),
    )
    return jax.shard_map(
        shards,
        mesh=mesh,
        in_specs=placed,
        out_specs=(P(("wide", "narrow"), None), P(None, ("wide", "narrow")), P()),
        check_vma=False,
    )
```

```python
import functools

import jax
import jax.numpy as jnp
from jax import lax
from jax.experimental import pallas as pl
from jax.experimental.pallas import tpu as pltpu
from jax.sharding import PartitionSpec as P


X, ZL, CORES = 4, 2, 2
Y, ZH = 4, 4
BOTH = ("wide", "narrow")


def narrow_perm(dx=0, flip_z=0, flip_core=0):
    pairs = []
    for x in range(X):
        for zl in range(ZL):
            for core in range(CORES):
                target = (((x + dx) % X) * ZL + (zl ^ flip_z)) * CORES + (core ^ flip_core)
                pairs.append(((x * ZL + zl) * CORES + core, target))
    return pairs


def wide_perm(dy=0, dz=0):
    return [
        (y * ZH + zh, ((y + dy) % Y) * ZH + (zh + dz) % ZH) for y in range(Y) for zh in range(ZH)
    ]


def to_narrow(value, **steps):
    return lax.ppermute(value, "narrow", narrow_perm(**steps))


def to_wide(value, **steps):
    return lax.ppermute(value, "wide", wide_perm(**steps))


SLOTS = 24
ORDER, COL, SRC, START, ROWS, DEST, OWN = 0, 24, 48, 72, 89, 105, 121
META = 128
GRANT = 60 * 1024 * 1024


def spmm_kernel(meta, normed, *refs):
    pieces, (sent, kept, own), (panel, blocks, acc, sem) = refs[:Y], refs[Y : Y + 3], refs[Y + 3 :]
    step = pl.program_id(0)
    rows = pl.num_programs(0) // 2
    width = panel.shape[2]

    @pl.when(step == 0)
    def _():
        copies = [pltpu.make_async_copy(normed, blocks, sem.at[Y * ZH])]
        for k in range(Y):
            for j in range(ZH):
                target = panel.at[meta[DEST + k * ZH + j]]
                copies.append(pltpu.make_async_copy(pieces[k].at[j], target, sem.at[k * ZH + j]))
        for copy in copies:
            copy.start()
        for copy in copies:
            copy.wait()
        own[...] = panel[meta[OWN]]

    row = meta[ROWS + step]
    first = meta[START + row]
    count = meta[START + row + 1] - first

    def product(at):
        slot = meta[ORDER + at]
        block = blocks[slot]
        clean = jnp.dot(block, panel[meta[COL + slot]], preferred_element_type=jnp.float32)
        corrupt = jnp.dot(block, panel[meta[SRC + slot]], preferred_element_type=jnp.float32)
        return clean, corrupt

    def write(out):
        @pl.when(count == 0)
        def _():
            out[...] = jnp.zeros_like(out)

        @pl.when(count == 1)
        def _():
            clean, corrupt = product(first)
            out[0, :, :width] = clean.astype(out.dtype)
            out[0, :, width:] = corrupt.astype(out.dtype)

        @pl.when(count > 1)
        def _():
            acc[:, :width], acc[:, width:] = product(first)

            def add_slot(at, carry):
                clean, corrupt = product(at)
                acc[:, :width] += clean
                acc[:, width:] += corrupt
                return carry

            lax.fori_loop(first + 1, first + count, add_slot, 0)
            out[0] = acc[...].astype(out.dtype)

    @pl.when(step < rows)
    def _():
        write(sent)

    @pl.when(step >= rows)
    def _():
        write(kept)


def spmm(meta, normed, pieces):
    slots, block_len, _ = normed.shape
    width = pieces[0].shape[2]
    rows = X * ZL
    half = jax.ShapeDtypeStruct((rows, block_len, 2 * width), jnp.bfloat16)
    return pl.pallas_call(
        spmm_kernel,
        grid=(2 * rows,),
        in_specs=[pl.BlockSpec(memory_space=pltpu.SMEM)]
        + [pl.BlockSpec(memory_space=pl.ANY)] * (1 + len(pieces)),
        out_specs=[
            pl.BlockSpec((1, block_len, 2 * width), lambda i: (jnp.minimum(i, rows - 1), 0, 0)),
            pl.BlockSpec((1, block_len, 2 * width), lambda i: (jnp.maximum(i - rows, 0), 0, 0)),
            pl.BlockSpec((block_len, width), lambda i: (0, 0)),
        ],
        out_shape=[half, half, jax.ShapeDtypeStruct((block_len, width), jnp.bfloat16)],
        scratch_shapes=[
            pltpu.VMEM((Y * ZH, block_len, width), jnp.bfloat16),
            pltpu.VMEM(normed.shape, normed.dtype),
            pltpu.VMEM((block_len, 2 * width), jnp.float32),
            pltpu.SemaphoreType.DMA((Y * ZH + 1,)),
        ],
        compiler_params=pltpu.CompilerParams(vmem_limit_bytes=GRANT),
        cost_estimate=pl.CostEstimate(
            flops=slots * block_len * block_len * 4 * width,
            bytes_accessed=10 * 1024 * 1024,
            transcendentals=0,
        ),
    )(meta, normed, *pieces)


def pair_kernel(kept, arrived, *outs):
    total = kept[...].astype(jnp.float32) + arrived[...].astype(jnp.float32)
    for k, out in enumerate(outs):
        out[...] = total[k].astype(out.dtype)


def pair_sum(kept, arrived):
    rows, block_len, width = kept.shape
    part = block_len // 2
    shape = (X, ZL, block_len, width)
    return pl.pallas_call(
        pair_kernel,
        grid=(ZL, 2),
        in_specs=[pl.BlockSpec((X, 1, part, width), lambda i, j: (0, i, j, 0))] * 2,
        out_specs=[pl.BlockSpec((1, part, width), lambda i, j: (i, j, 0))] * X,
        out_shape=[jax.ShapeDtypeStruct(shape[1:], jnp.bfloat16)] * X,
        compiler_params=pltpu.CompilerParams(vmem_limit_bytes=GRANT),
        cost_estimate=pl.CostEstimate(
            flops=rows * block_len * width,
            bytes_accessed=6 * rows * block_len * width,
            transcendentals=0,
        ),
    )(kept.reshape(shape), arrived.reshape(shape))


def finish_kernel(parts, width, degree, bias, own, own_corrupt, *refs):
    ins, (clean, corrupt, hidden, spread) = refs[:-4], refs[-4:]
    for at in range(len(ins) // (parts + 1)):
        group = ins[at * (parts + 1) : (at + 1) * (parts + 1)]
        total = group[parts][...].astype(jnp.float32)
        for ref in group[:parts]:
            total += ref[0].astype(jnp.float32)
        columns = slice(at * width, (at + 1) * width)
        inner = slice(0, width)
        for out, value, source in (
            (clean, total[:, :width], own[:, columns]),
            (corrupt, total[:, width:], own_corrupt[at][:, inner]),
        ):
            value = value + source.astype(jnp.float32) / degree[...] + bias[:, columns]
            out[:, columns] = jnp.maximum(value, 0.0)
    final = clean[...]
    hidden[...] = final.astype(hidden.dtype)
    sums = jnp.sum(final, axis=0, keepdims=True).astype(spread.dtype)
    spread[...] = jnp.broadcast_to(sums, spread.shape)


def finish(devices, degree, bias, own, own_corrupt, groups):
    block_len, hidden = own.shape
    width = hidden // len(groups)
    parts = len(groups[0]) - 1
    near = pl.BlockSpec((1, block_len, 2 * width), lambda i: (0, 0, 0))
    last = pl.BlockSpec((block_len, 2 * width), lambda i: (0, 0))

    def whole(*shape):
        return pl.BlockSpec(shape, lambda i: (0,) * len(shape))

    return pl.pallas_call(
        functools.partial(finish_kernel, parts, width),
        grid=(1,),
        in_specs=[
            whole(block_len, 1),
            whole(1, hidden),
            whole(block_len, hidden),
            whole(len(groups), block_len, width),
        ]
        + ([near] * parts + [last]) * len(groups),
        out_specs=[whole(block_len, hidden)] * 3 + [whole(devices, hidden)],
        out_shape=[
            jax.ShapeDtypeStruct((block_len, hidden), jnp.float32),
            jax.ShapeDtypeStruct((block_len, hidden), jnp.float32),
            jax.ShapeDtypeStruct((block_len, hidden), jnp.bfloat16),
            jax.ShapeDtypeStruct((devices, hidden), jnp.bfloat16),
        ],
        compiler_params=pltpu.CompilerParams(vmem_limit_bytes=GRANT),
    )(degree, bias, own, own_corrupt, *[value for group in groups for value in group])


def score_kernel(nodes, gathered, disc_weight, clean, corrupt, scores, spread):
    column_total = jnp.sum(gathered[...].astype(jnp.float32), axis=0, keepdims=True)
    summary = jax.nn.sigmoid(column_total / nodes)
    lanes = (((1,), (1,)), ((), ()))
    exact = dict(precision=lax.Precision.HIGHEST, preferred_element_type=jnp.float32)
    summary = jnp.broadcast_to(summary, (8, summary.shape[1]))
    probe = lax.dot_general(summary, disc_weight[...], lanes, **exact)
    clean_score = lax.dot_general(probe, clean[...], lanes, **exact)[:1]
    corrupt_score = lax.dot_general(probe, corrupt[...], lanes, **exact)[:1]
    scores[0:1] = clean_score
    scores[1:2] = corrupt_score

    def softplus(value):
        return jnp.maximum(value, 0.0) + jnp.log1p(jnp.exp(-jnp.abs(value)))

    terms = softplus(-clean_score) + softplus(corrupt_score)
    spread[...] = jnp.broadcast_to(jnp.sum(terms, axis=1, keepdims=True), spread.shape)


def score(nodes, devices, gathered, disc_weight, clean, corrupt):
    block_len = clean.shape[0]
    return pl.pallas_call(
        functools.partial(score_kernel, nodes),
        out_shape=[
            jax.ShapeDtypeStruct((2, block_len), jnp.float32),
            jax.ShapeDtypeStruct((devices, 128), jnp.float32),
        ],
        compiler_params=pltpu.CompilerParams(vmem_limit_bytes=GRANT),
    )(gathered, disc_weight, clean, corrupt)


def step(
    features,
    proj_weight,
    bias,
    disc_weight,
    adjacency,
    row_block,
    col_block,
    block_count,
    degree,
    corrupt_source,
):
    block_len = adjacency.shape[-1]
    hidden = proj_weight.shape[1]
    wide_size = lax.axis_size("wide")
    narrow_size = lax.axis_size("narrow")
    devices = wide_size * narrow_size
    wide_at = lax.axis_index("wide")
    narrow_at = lax.axis_index("narrow")
    y, zh = wide_at // ZH, wide_at % ZH
    x, zl, core = narrow_at // (ZL * CORES), narrow_at // CORES % ZL, narrow_at % CORES
    chunks = 2
    width = hidden // chunks

    own = []
    panels = []
    for h in range(chunks):
        weight = proj_weight[:, h * width : (h + 1) * width]
        part = jnp.dot(features, weight, preferred_element_type=jnp.float32)
        part = part.astype(jnp.bfloat16)
        own.append(part)
        along_z = [part] + [to_wide(part, dz=k) for k in range(1, ZH)]
        along_z = jnp.stack(along_z)
        panels.append([along_z] + [to_wide(along_z, dy=k) for k in range(1, Y)])

    inv_root = lax.rsqrt(degree.astype(jnp.float32))
    col_roots = lax.dynamic_index_in_dim(
        inv_root.reshape(wide_size, narrow_size, block_len), narrow_at, 1, keepdims=False
    )
    row_roots = lax.dynamic_index_in_dim(
        inv_root.reshape(wide_size, narrow_size, block_len), wide_at, 0, keepdims=False
    )
    slot_rows = row_block[0, 0]
    slot_cols = col_block[0, 0]
    normed = (
        adjacency[0, 0].astype(jnp.float32)
        * row_roots[slot_rows][:, :, None]
        * col_roots[slot_cols][:, None, :]
    ).astype(jnp.bfloat16)

    slot_ids = jnp.arange(SLOTS, dtype=jnp.int32)
    keys = jnp.where(slot_ids < block_count[0, 0], slot_rows, narrow_size)
    before = (keys[None, :] < keys[:, None]) | (
        (keys[None, :] == keys[:, None]) & (slot_ids[None, :] < slot_ids[:, None])
    )
    rank = jnp.sum(before.astype(jnp.int32), axis=1)
    order = jnp.sum(jnp.where(rank[None, :] == slot_ids[:, None], slot_ids[None, :], 0), axis=1)
    starts = jnp.sum(
        (keys[None, :] < jnp.arange(narrow_size + 1, dtype=jnp.int32)[:, None]).astype(jnp.int32),
        axis=1,
    )
    columns = jnp.arange(wide_size, dtype=jnp.int32)
    sources = (
        lax.dynamic_index_in_dim(
            corrupt_source.reshape(wide_size, narrow_size), narrow_at, 1, keepdims=False
        )
        // narrow_size
    )
    slot_sources = jnp.sum(
        jnp.where(slot_cols[:, None] == columns[None, :], sources[None, :], 0), axis=1
    )
    own_source = jnp.sum(jnp.where(columns == wide_at, sources, 0))
    steps_x = jnp.arange(X, dtype=jnp.int32)
    flips = jnp.arange(ZL, dtype=jnp.int32)
    targets = ((x + steps_x)[:, None] % X * ZL + (zl ^ flips)[None, :]) * CORES
    dest = (y - jnp.arange(Y, dtype=jnp.int32))[:, None] % Y * ZH + (
        zh - jnp.arange(ZH, dtype=jnp.int32)
    )[None, :] % ZH
    parts = [
        order,
        slot_cols,
        slot_sources,
        starts,
        (targets + 1 - core).reshape(-1),
        (targets + core).reshape(-1),
        dest.reshape(-1),
        own_source[None],
    ]
    parts.append(jnp.zeros((META - sum(part.shape[0] for part in parts),), jnp.int32))
    meta = jnp.concatenate([part.astype(jnp.int32) for part in parts])

    own_corrupt = []
    groups = []
    for h in range(chunks):
        sent, kept, own_part = spmm(meta, normed, panels[h])
        own_corrupt.append(own_part)
        arrived = to_narrow(sent, flip_core=1)
        halves = pair_sum(kept, arrived)
        got = [halves[0]] + [to_narrow(halves[k], dx=k) for k in range(1, X)]
        far = sum(value[1].astype(jnp.float32) for value in got).astype(jnp.bfloat16)
        last = to_narrow(far, flip_z=1)
        groups.append(got + [last])

    own_degree = lax.dynamic_index_in_dim(
        degree.reshape(devices, block_len), wide_at * narrow_size + narrow_at, 0, keepdims=False
    )
    degree_float = own_degree.astype(jnp.float32)[:, None]
    nodes = block_len * devices
    clean_h, corrupt_h, hidden_out, spread = finish(
        devices,
        degree_float,
        bias[None, :],
        jnp.concatenate(own, axis=1),
        jnp.stack(own_corrupt),
        groups,
    )
    gathered = lax.all_to_all(spread, BOTH, 0, 0, tiled=True)
    scores, spread = score(nodes, devices, gathered, disc_weight, clean_h, corrupt_h)
    gathered = lax.all_to_all(spread, BOTH, 0, 0, tiled=True)
    loss = jnp.sum(gathered[:, 0]) / (2 * nodes)
    return (hidden_out, scores, loss)


def solution(mesh):
    placed = (
        P(("wide", "narrow"), None),
        P(),
        P(),
        P(),
        P("wide", "narrow", None, None, None),
        P("wide", "narrow", None),
        P("wide", "narrow", None),
        P("wide", "narrow"),
        P(),
        P(),
    )
    return jax.shard_map(
        step,
        mesh=mesh,
        in_specs=placed,
        out_specs=(P(("wide", "narrow"), None), P(None, ("wide", "narrow")), P()),
        check_vma=False,
    )
```

```python
import functools

import jax
import jax.numpy as jnp
from jax import lax
from jax.experimental import pallas as pl
from jax.experimental.pallas import tpu as pltpu
from jax.sharding import PartitionSpec as P


X, ZL, CORES = 4, 2, 2
Y, ZH = 4, 4
BOTH = ("wide", "narrow")


def narrow_perm(dx=0, flip_z=0, flip_core=0):
    pairs = []
    for x in range(X):
        for zl in range(ZL):
            for core in range(CORES):
                target = (((x + dx) % X) * ZL + (zl ^ flip_z)) * CORES + (core ^ flip_core)
                pairs.append(((x * ZL + zl) * CORES + core, target))
    return pairs


def wide_perm(dy=0, dz=0):
    return [
        (y * ZH + zh, ((y + dy) % Y) * ZH + (zh + dz) % ZH) for y in range(Y) for zh in range(ZH)
    ]


def to_narrow(value, **steps):
    return lax.ppermute(value, "narrow", narrow_perm(**steps))


def to_wide(value, **steps):
    return lax.ppermute(value, "wide", wide_perm(**steps))


SLOTS = 24
ORDER, COL, SRC, START, ROWS, DEST, OWN = 0, 24, 48, 72, 89, 105, 121
META = 128
LANES = 128
GRANT = 60 * 1024 * 1024


def spmm_kernel(meta, normed, *refs):
    pieces, (sent, kept, own) = refs[:Y], refs[Y : Y + 3]
    panel, blocks, result, acc, sem_in, sem_out = refs[Y + 3 :]
    rows = sent.shape[0]
    width = panel.shape[2]

    copies = [pltpu.make_async_copy(normed, blocks, sem_in.at[Y * ZH])]
    for k in range(Y):
        for j in range(ZH):
            target = panel.at[meta[DEST + k * ZH + j]]
            copies.append(pltpu.make_async_copy(pieces[k].at[j], target, sem_in.at[k * ZH + j]))
    for copy in copies:
        copy.start()
    for copy in copies:
        copy.wait()
    own_copy = pltpu.make_async_copy(panel.at[meta[OWN]], own, sem_out.at[2 * rows])
    own_copy.start()

    def product(at):
        slot = meta[ORDER + at]
        block = blocks[slot]
        clean = jnp.dot(block, panel[meta[COL + slot]], preferred_element_type=jnp.float32)
        corrupt = jnp.dot(block, panel[meta[SRC + slot]], preferred_element_type=jnp.float32)
        return clean, corrupt

    def make_row(step):
        row = meta[ROWS + step]
        first = meta[START + row]
        count = meta[START + row + 1] - first

        @pl.when(count == 0)
        def _():
            result[step] = jnp.zeros(result.shape[1:], result.dtype)

        @pl.when(count == 1)
        def _():
            clean, corrupt = product(first)
            result[step, :, :width] = clean.astype(result.dtype)
            result[step, :, width:] = corrupt.astype(result.dtype)

        @pl.when(count > 1)
        def _():
            acc[:, :width], acc[:, width:] = product(first)

            def add_slot(at, carry):
                clean, corrupt = product(at)
                acc[:, :width] += clean
                acc[:, width:] += corrupt
                return carry

            lax.fori_loop(first + 1, first + count, add_slot, 0)
            result[step] = acc[...].astype(result.dtype)

    def leave(step, out, at):
        return pltpu.make_async_copy(result.at[step], out.at[at], sem_out.at[step])

    def send_row(step, carry):
        make_row(step)
        leave(step, sent, step).start()
        return carry

    def keep_row(step, carry):
        make_row(step)
        leave(step, kept, step - rows).start()
        return carry

    lax.fori_loop(0, rows, send_row, 0)
    lax.fori_loop(rows, 2 * rows, keep_row, 0)
    own_copy.wait()
    for step in range(rows):
        leave(step, sent, step).wait()
        leave(rows + step, kept, step).wait()


def spmm(meta, normed, pieces):
    slots, block_len, _ = normed.shape
    width = pieces[0].shape[2]
    rows = X * ZL
    half = jax.ShapeDtypeStruct((rows, block_len, 2 * width), jnp.bfloat16)
    return pl.pallas_call(
        spmm_kernel,
        in_specs=[pl.BlockSpec(memory_space=pltpu.SMEM)]
        + [pl.BlockSpec(memory_space=pl.ANY)] * (1 + len(pieces)),
        out_specs=[pl.BlockSpec(memory_space=pl.ANY)] * 3,
        out_shape=[half, half, jax.ShapeDtypeStruct((block_len, width), jnp.bfloat16)],
        scratch_shapes=[
            pltpu.VMEM((Y * ZH, block_len, width), jnp.bfloat16),
            pltpu.VMEM(normed.shape, normed.dtype),
            pltpu.VMEM((2 * rows, block_len, 2 * width), jnp.bfloat16),
            pltpu.VMEM((block_len, 2 * width), jnp.float32),
            pltpu.SemaphoreType.DMA((Y * ZH + 1,)),
            pltpu.SemaphoreType.DMA((2 * rows + 1,)),
        ],
        compiler_params=pltpu.CompilerParams(vmem_limit_bytes=GRANT),
        cost_estimate=pl.CostEstimate(
            flops=slots * block_len * block_len * 4 * width,
            bytes_accessed=10 * 1024 * 1024,
            transcendentals=0,
        ),
    )(meta, normed, *pieces)


def pair_kernel(kept, arrived, *refs):
    outs, (mine, theirs, sem_mine, sem_theirs, sem_out) = refs[:X], refs[X:]
    order = [(k, f) for k in [*range(1, X), 0] for f in range(ZL)]

    def load(source, target, sem, k, f):
        at = k * ZL + f
        return pltpu.make_async_copy(source.at[at], target.at[at], sem.at[at])

    def leave(k, f):
        at = k * ZL + f
        return pltpu.make_async_copy(mine.at[at], outs[k].at[f], sem_out.at[at])

    for k, f in order:
        load(kept, mine, sem_mine, k, f).start()
        load(arrived, theirs, sem_theirs, k, f).start()
    for k, f in order:
        at = k * ZL + f
        load(kept, mine, sem_mine, k, f).wait()
        load(arrived, theirs, sem_theirs, k, f).wait()
        total = mine[at].astype(jnp.float32) + theirs[at].astype(jnp.float32)
        mine[at] = total.astype(mine.dtype)
        leave(k, f).start()
    for k, f in order:
        leave(k, f).wait()


def pair_sum(kept, arrived):
    rows, block_len, width = kept.shape
    return pl.pallas_call(
        pair_kernel,
        in_specs=[pl.BlockSpec(memory_space=pl.ANY)] * 2,
        out_specs=[pl.BlockSpec(memory_space=pl.ANY)] * X,
        out_shape=[jax.ShapeDtypeStruct((ZL, block_len, width), jnp.bfloat16)] * X,
        scratch_shapes=[
            pltpu.VMEM(kept.shape, kept.dtype),
            pltpu.VMEM(kept.shape, kept.dtype),
            pltpu.SemaphoreType.DMA((rows,)),
            pltpu.SemaphoreType.DMA((rows,)),
            pltpu.SemaphoreType.DMA((rows,)),
        ],
        compiler_params=pltpu.CompilerParams(vmem_limit_bytes=GRANT),
        cost_estimate=pl.CostEstimate(
            flops=rows * block_len * width,
            bytes_accessed=6 * rows * block_len * width,
            transcendentals=0,
        ),
    )(kept, arrived)


def finish_kernel(parts, width, degree, bias, own, own_corrupt, *refs):
    ins, (clean, corrupt, hidden, spread) = refs[:-4], refs[-4:]
    for at in range(len(ins) // (parts + 1)):
        group = ins[at * (parts + 1) : (at + 1) * (parts + 1)]
        total = group[parts][...].astype(jnp.float32)
        for ref in group[:parts]:
            total += ref[0].astype(jnp.float32)
        columns = slice(at * width, (at + 1) * width)
        inner = slice(0, width)
        for out, value, source in (
            (clean, total[:, :width], own[:, columns]),
            (corrupt, total[:, width:], own_corrupt[at][:, inner]),
        ):
            value = value + source.astype(jnp.float32) / degree[...] + bias[:, columns]
            out[:, columns] = jnp.maximum(value, 0.0)
    final = clean[...]
    hidden[...] = final.astype(hidden.dtype)
    sums = jnp.sum(final, axis=0, keepdims=True).astype(spread.dtype)
    for at in range(spread.shape[1]):
        part = sums[:, at * LANES : (at + 1) * LANES][None]
        spread[:, at : at + 1, :] = jnp.broadcast_to(part, (spread.shape[0], 1, LANES))


def finish(devices, degree, bias, own, own_corrupt, groups):
    block_len, hidden = own.shape
    width = hidden // len(groups)
    parts = len(groups[0]) - 1
    near = pl.BlockSpec((1, block_len, 2 * width), lambda i: (0, 0, 0))
    last = pl.BlockSpec((block_len, 2 * width), lambda i: (0, 0))

    def whole(*shape):
        return pl.BlockSpec(shape, lambda i: (0,) * len(shape))

    return pl.pallas_call(
        functools.partial(finish_kernel, parts, width),
        grid=(1,),
        in_specs=[
            whole(block_len, 1),
            whole(1, hidden),
            whole(block_len, hidden),
            whole(len(groups), block_len, width),
        ]
        + ([near] * parts + [last]) * len(groups),
        out_specs=[whole(block_len, hidden)] * 3 + [whole(devices, hidden // LANES, LANES)],
        out_shape=[
            jax.ShapeDtypeStruct((block_len, hidden), jnp.float32),
            jax.ShapeDtypeStruct((block_len, hidden), jnp.float32),
            jax.ShapeDtypeStruct((block_len, hidden), jnp.bfloat16),
            jax.ShapeDtypeStruct((devices, hidden // LANES, LANES), jnp.bfloat16),
        ],
        compiler_params=pltpu.CompilerParams(vmem_limit_bytes=GRANT),
    )(degree, bias, own, own_corrupt, *[value for group in groups for value in group])


def score_kernel(nodes, gathered, disc_weight, clean, corrupt, scores, spread):
    column_total = jnp.sum(gathered[...].astype(jnp.float32), axis=0)
    pieces = [column_total[at : at + 1] for at in range(column_total.shape[0])]
    summary = jax.nn.sigmoid(jnp.concatenate(pieces, axis=1) / nodes)
    lanes = (((1,), (1,)), ((), ()))
    exact = dict(precision=lax.Precision.HIGHEST, preferred_element_type=jnp.float32)
    summary = jnp.broadcast_to(summary, (8, summary.shape[1]))
    probe = lax.dot_general(summary, disc_weight[...], lanes, **exact)
    clean_score = lax.dot_general(probe, clean[...], lanes, **exact)[:1]
    corrupt_score = lax.dot_general(probe, corrupt[...], lanes, **exact)[:1]
    scores[0:1] = clean_score
    scores[1:2] = corrupt_score

    def softplus(value):
        return jnp.maximum(value, 0.0) + jnp.log1p(jnp.exp(-jnp.abs(value)))

    terms = softplus(-clean_score) + softplus(corrupt_score)
    spread[...] = jnp.broadcast_to(jnp.sum(terms, axis=1, keepdims=True), spread.shape)


def score(nodes, devices, gathered, disc_weight, clean, corrupt):
    block_len = clean.shape[0]
    return pl.pallas_call(
        functools.partial(score_kernel, nodes),
        out_shape=[
            jax.ShapeDtypeStruct((2, block_len), jnp.float32),
            jax.ShapeDtypeStruct((devices, 128), jnp.float32),
        ],
        compiler_params=pltpu.CompilerParams(vmem_limit_bytes=GRANT),
    )(gathered, disc_weight, clean, corrupt)


def infomax(
    features,
    proj_weight,
    bias,
    disc_weight,
    adjacency,
    row_block,
    col_block,
    block_count,
    degree,
    corrupt_source,
):
    block_len = adjacency.shape[-1]
    hidden = proj_weight.shape[1]
    wide_size = lax.axis_size("wide")
    narrow_size = lax.axis_size("narrow")
    devices = wide_size * narrow_size
    wide_at = lax.axis_index("wide")
    narrow_at = lax.axis_index("narrow")
    y, zh = wide_at // ZH, wide_at % ZH
    x, zl, core = narrow_at // (ZL * CORES), narrow_at // CORES % ZL, narrow_at % CORES
    chunks = 2
    width = hidden // chunks

    own = []
    panels = []
    for h in range(chunks):
        weight = proj_weight[:, h * width : (h + 1) * width]
        part = jnp.dot(features, weight, preferred_element_type=jnp.float32)
        part = part.astype(jnp.bfloat16)
        own.append(part)
        along_z = [part]
        for k in range(1, ZH):
            along_z.append(to_wide(part, dz=k))
        along_z = jnp.stack(along_z)
        panel = [along_z]
        for k in range(1, Y):
            panel.append(to_wide(along_z, dy=k))
        panels.append(panel)

    inv_root = lax.rsqrt(degree.astype(jnp.float32))
    col_roots = lax.dynamic_index_in_dim(
        inv_root.reshape(wide_size, narrow_size, block_len), narrow_at, 1, keepdims=False
    )
    row_roots = lax.dynamic_index_in_dim(
        inv_root.reshape(wide_size, narrow_size, block_len), wide_at, 0, keepdims=False
    )
    slot_rows = row_block[0, 0]
    slot_cols = col_block[0, 0]
    normed = (
        adjacency[0, 0].astype(jnp.float32)
        * row_roots[slot_rows][:, :, None]
        * col_roots[slot_cols][:, None, :]
    ).astype(jnp.bfloat16)

    slot_ids = jnp.arange(SLOTS, dtype=jnp.int32)
    keys = jnp.where(slot_ids < block_count[0, 0], slot_rows, narrow_size)
    before = (keys[None, :] < keys[:, None]) | (
        (keys[None, :] == keys[:, None]) & (slot_ids[None, :] < slot_ids[:, None])
    )
    rank = jnp.sum(before.astype(jnp.int32), axis=1)
    order = jnp.sum(jnp.where(rank[None, :] == slot_ids[:, None], slot_ids[None, :], 0), axis=1)
    starts = jnp.sum(
        (keys[None, :] < jnp.arange(narrow_size + 1, dtype=jnp.int32)[:, None]).astype(jnp.int32),
        axis=1,
    )
    columns = jnp.arange(wide_size, dtype=jnp.int32)
    sources = (
        lax.dynamic_index_in_dim(
            corrupt_source.reshape(wide_size, narrow_size), narrow_at, 1, keepdims=False
        )
        // narrow_size
    )
    slot_sources = jnp.sum(
        jnp.where(slot_cols[:, None] == columns[None, :], sources[None, :], 0), axis=1
    )
    own_source = jnp.sum(jnp.where(columns == wide_at, sources, 0))
    steps_x = jnp.arange(X, dtype=jnp.int32)
    flips = jnp.arange(ZL, dtype=jnp.int32)
    targets = ((x + steps_x)[:, None] % X * ZL + (zl ^ flips)[None, :]) * CORES
    dest = (y - jnp.arange(Y, dtype=jnp.int32))[:, None] % Y * ZH + (
        zh - jnp.arange(ZH, dtype=jnp.int32)
    )[None, :] % ZH
    parts = [
        order,
        slot_cols,
        slot_sources,
        starts,
        (targets + 1 - core).reshape(-1),
        (targets + core).reshape(-1),
        dest.reshape(-1),
        own_source[None],
    ]
    parts.append(jnp.zeros((META - sum(part.shape[0] for part in parts),), jnp.int32))
    meta = jnp.concatenate([part.astype(jnp.int32) for part in parts])

    own_corrupt = []
    groups = []
    for h in range(chunks):
        sent, kept, own_part = spmm(meta, normed, panels[h])
        own_corrupt.append(own_part)
        arrived = to_narrow(sent, flip_core=1)
        halves = pair_sum(kept, arrived)
        got = [halves[0]]
        for k in range(1, X):
            got.append(to_narrow(halves[k], dx=k))
        far = sum(value[1].astype(jnp.float32) for value in got).astype(jnp.bfloat16)
        last = to_narrow(far, flip_z=1)
        groups.append(got + [last])

    own_degree = lax.dynamic_index_in_dim(
        degree.reshape(devices, block_len), wide_at * narrow_size + narrow_at, 0, keepdims=False
    )
    degree_float = own_degree.astype(jnp.float32)[:, None]
    nodes = block_len * devices
    clean_h, corrupt_h, hidden_out, spread = finish(
        devices,
        degree_float,
        bias[None, :],
        jnp.concatenate(own, axis=1),
        jnp.stack(own_corrupt),
        groups,
    )
    gathered = lax.all_to_all(spread, BOTH, 0, 0)
    scores, spread = score(nodes, devices, gathered, disc_weight, clean_h, corrupt_h)
    gathered = lax.all_to_all(spread, BOTH, 0, 0, tiled=True)
    loss = jnp.sum(gathered[:, 0]) / (2 * nodes)
    return (hidden_out, scores, loss)


def solution(mesh):
    placed = (
        P(("wide", "narrow"), None),
        P(),
        P(),
        P(),
        P("wide", "narrow", None, None, None),
        P("wide", "narrow", None),
        P("wide", "narrow", None),
        P("wide", "narrow"),
        P(),
        P(),
    )
    return jax.shard_map(
        infomax,
        mesh=mesh,
        in_specs=placed,
        out_specs=(P(("wide", "narrow"), None), P(None, ("wide", "narrow")), P()),
        check_vma=False,
    )
```

```python
import functools

import jax
import jax.numpy as jnp
from jax import lax
from jax.experimental import pallas as pl
from jax.experimental.pallas import tpu as pltpu
from jax.sharding import PartitionSpec as P


X, ZL, CORES = 4, 2, 2
Y, ZH = 4, 4
BOTH = ("wide", "narrow")


def narrow_perm(dx=0, flip_z=0, flip_core=0):
    pairs = []
    for x in range(X):
        for zl in range(ZL):
            for core in range(CORES):
                target = (((x + dx) % X) * ZL + (zl ^ flip_z)) * CORES + (core ^ flip_core)
                pairs.append(((x * ZL + zl) * CORES + core, target))
    return pairs


def wide_perm(dy=0, dz=0):
    return [
        (y * ZH + zh, ((y + dy) % Y) * ZH + (zh + dz) % ZH) for y in range(Y) for zh in range(ZH)
    ]


def to_narrow(value, **steps):
    return lax.ppermute(value, "narrow", narrow_perm(**steps))


def to_wide(value, **steps):
    return lax.ppermute(value, "wide", wide_perm(**steps))


SLOTS = 24
ORDER, COL, SRC, START, ROWS, DEST, OWN = 0, 48, 96, 144, 161, 169, 185
META = 256
LANES = 128
MIB = 1024 * 1024


def products_kernel(split, meta, normed, other_normed, *refs):
    pieces, refs = refs[: 2 * Y], refs[2 * Y :]
    sides, refs = refs[: ZL * split], refs[ZL * split :]
    outs, own = refs[:X], refs[X]
    panel, blocks, result, acc, sem_panel, sem_block, sem_out = refs[X + 1 :]
    rows = X * ZL
    width = panel.shape[2]

    copies = []
    for k in range(Y):
        for j in range(ZH):
            at = meta[DEST + k * ZH + j]
            for core in range(CORES):
                copies.append(
                    pltpu.make_async_copy(
                        pieces[core * Y + k].at[j],
                        panel.at[core * Y * ZH + at],
                        sem_panel.at[(k * ZH + j) * CORES + core],
                    )
                )
    for copy in copies:
        copy.start()

    def span(step):
        row = meta[ROWS + step]
        return meta[START + row], meta[START + row + 1]

    def fetch_row(step, carry):
        def fetch(at, carry):
            slot = meta[ORDER + at]

            @pl.when(slot < SLOTS)
            def _():
                pltpu.make_async_copy(normed.at[slot], blocks.at[slot], sem_block.at[slot]).start()

            @pl.when(slot >= SLOTS)
            def _():
                pltpu.make_async_copy(
                    other_normed.at[slot - SLOTS], blocks.at[slot], sem_block.at[slot]
                ).start()

            return carry

        return lax.fori_loop(*span(step), fetch, carry)

    lax.fori_loop(0, rows, fetch_row, 0)
    for copy in copies:
        copy.wait()
    own_copy = pltpu.make_async_copy(panel.at[meta[OWN]], own, sem_out.at[2 * rows])
    own_copy.start()

    def product(at):
        slot = meta[ORDER + at]
        pltpu.make_async_copy(normed.at[0], blocks.at[slot], sem_block.at[slot]).wait()
        block = blocks[slot]
        clean = jnp.dot(block, panel[meta[COL + slot]], preferred_element_type=jnp.float32)
        corrupt = jnp.dot(block, panel[meta[SRC + slot]], preferred_element_type=jnp.float32)
        return clean, corrupt

    def make_row(step):
        first, end = span(step)
        count = end - first

        @pl.when(count == 0)
        def _():
            result[step] = jnp.zeros(result.shape[1:], result.dtype)

        @pl.when(count == 1)
        def _():
            clean, corrupt = product(first)
            result[step, :, :width] = clean.astype(result.dtype)
            result[step, :, width:] = corrupt.astype(result.dtype)

        @pl.when(count > 1)
        def _():
            acc[:, :width], acc[:, width:] = product(first)

            def add_slot(at, carry):
                clean, corrupt = product(at)
                acc[:, :width] += clean
                acc[:, width:] += corrupt
                return carry

            lax.fori_loop(first + 1, end, add_slot, 0)
            result[step] = acc[...].astype(result.dtype)

    def leave(k, f):
        step = k * ZL + f
        row = result.at[step]
        if not split:
            return [pltpu.make_async_copy(row, outs[k].at[f], sem_out.at[step])]
        clean, corrupt = row.at[:, pl.ds(0, width)], row.at[:, pl.ds(width, width)]
        return [
            pltpu.make_async_copy(clean, sides[f].at[k], sem_out.at[step]),
            pltpu.make_async_copy(corrupt, outs[k].at[f], sem_out.at[rows + step]),
        ]

    def emit(step, carry):
        make_row(step)
        for k in range(X):
            for f in range(ZL):

                @pl.when(step == k * ZL + f)
                def _(k=k, f=f):
                    for copy in leave(k, f):
                        copy.start()

        return carry

    lax.fori_loop(0, rows, emit, 0)
    own_copy.wait()
    for k in range(X):
        for f in range(ZL):
            for copy in leave(k, f):
                copy.wait()


def products(split, meta, normed, other_normed, pieces):
    slots, block_len, _ = normed.shape
    width = pieces[0].shape[2]
    outs = [jax.ShapeDtypeStruct((ZL, block_len, width if split else 2 * width), jnp.bfloat16)] * X
    if split:
        outs = [jax.ShapeDtypeStruct((X, block_len, width), jnp.bfloat16)] * ZL + outs
    return pl.pallas_call(
        functools.partial(products_kernel, split),
        in_specs=[pl.BlockSpec(memory_space=pltpu.SMEM)]
        + [pl.BlockSpec(memory_space=pl.ANY)] * (2 + len(pieces)),
        out_specs=[pl.BlockSpec(memory_space=pl.ANY)] * (len(outs) + 1),
        out_shape=outs + [jax.ShapeDtypeStruct((block_len, width), jnp.bfloat16)],
        scratch_shapes=[
            pltpu.VMEM((CORES * Y * ZH, block_len, width), jnp.bfloat16),
            pltpu.VMEM((CORES * slots, block_len, block_len), normed.dtype),
            pltpu.VMEM((X * ZL, block_len, 2 * width), jnp.bfloat16),
            pltpu.VMEM((block_len, 2 * width), jnp.float32),
            pltpu.SemaphoreType.DMA((CORES * Y * ZH,)),
            pltpu.SemaphoreType.DMA((CORES * slots,)),
            pltpu.SemaphoreType.DMA((2 * X * ZL + 1,)),
        ],
        compiler_params=pltpu.CompilerParams(vmem_limit_bytes=60 * MIB),
        cost_estimate=pl.CostEstimate(
            flops=slots * block_len * block_len * 4 * width,
            bytes_accessed=10 * MIB,
            transcendentals=0,
        ),
    )(meta, normed, other_normed, *pieces)


def finish_kernel(degree, bias, *refs):
    joint, apart, (clean, corrupt, hidden, spread) = refs[: X + 3], refs[X + 3 : -4], refs[-4:]
    scale = degree[...]
    offset = bias[...]

    def total(values):
        result = values[0].astype(jnp.float32)
        for value in values[1:]:
            result += value.astype(jnp.float32)
        return result

    def write(out, sums, own, columns):
        value = sums + own[...].astype(jnp.float32) / scale + offset[:, columns]
        out[:, columns] = jnp.maximum(value, 0.0)

    *parts, last, own, own_corrupt = joint
    width = own.shape[1]
    sums = total([ref[0] for ref in parts] + [last[...]])
    write(clean, sums[:, :width], own, slice(0, width))
    write(corrupt, sums[:, width:], own_corrupt, slice(0, width))
    parts, (last, own, own_corrupt) = apart[: 2 * X], apart[2 * X :]
    write(clean, total([ref[...] for ref in parts[:X]]), own, slice(width, 2 * width))
    sums = total([ref[0] for ref in parts[X:]] + [last[...]])
    write(corrupt, sums, own_corrupt, slice(width, 2 * width))
    final = clean[...]
    hidden[...] = final.astype(hidden.dtype)
    sums = jnp.sum(final, axis=0, keepdims=True).astype(spread.dtype)
    for at in range(spread.shape[1]):
        part = sums[:, at * LANES : (at + 1) * LANES][None]
        spread[:, at : at + 1, :] = jnp.broadcast_to(part, (spread.shape[0], 1, LANES))


def finish(devices, degree, bias, joint, apart):
    block_len, hidden = degree.shape[0], bias.shape[1]
    width = hidden // 2

    def whole(*shape):
        return pl.BlockSpec(shape, lambda i: (0,) * len(shape))

    half = [whole(block_len, width)]
    return pl.pallas_call(
        finish_kernel,
        grid=(1,),
        in_specs=[whole(block_len, 1), whole(1, hidden)]
        + [whole(1, block_len, hidden)] * X
        + [whole(block_len, hidden)]
        + half * (2 + X)
        + [whole(1, block_len, width)] * X
        + half * 3,
        out_specs=[whole(block_len, hidden)] * 3 + [whole(devices, hidden // LANES, LANES)],
        out_shape=[
            jax.ShapeDtypeStruct((block_len, hidden), jnp.float32),
            jax.ShapeDtypeStruct((block_len, hidden), jnp.float32),
            jax.ShapeDtypeStruct((block_len, hidden), jnp.bfloat16),
            jax.ShapeDtypeStruct((devices, hidden // LANES, LANES), jnp.bfloat16),
        ],
        compiler_params=pltpu.CompilerParams(vmem_limit_bytes=60 * MIB),
    )(degree, bias, *joint, *apart)


def score_kernel(nodes, gathered, disc_weight, clean, corrupt, scores, spread):
    column_total = jnp.sum(gathered[...].astype(jnp.float32), axis=0)
    pieces = [column_total[at : at + 1] for at in range(column_total.shape[0])]
    summary = jax.nn.sigmoid(jnp.concatenate(pieces, axis=1) / nodes)
    lanes = (((1,), (1,)), ((), ()))
    exact = dict(precision=lax.Precision.HIGHEST, preferred_element_type=jnp.float32)
    summary = jnp.broadcast_to(summary, (8, summary.shape[1]))
    probe = lax.dot_general(summary, disc_weight[...], lanes, **exact)
    clean_score = lax.dot_general(probe, clean[...], lanes, **exact)[:1]
    corrupt_score = lax.dot_general(probe, corrupt[...], lanes, **exact)[:1]
    scores[0:1] = clean_score
    scores[1:2] = corrupt_score

    def softplus(value):
        return jnp.maximum(value, 0.0) + jnp.log1p(jnp.exp(-jnp.abs(value)))

    terms = softplus(-clean_score) + softplus(corrupt_score)
    spread[...] = jnp.broadcast_to(jnp.sum(terms, axis=1, keepdims=True), spread.shape)


def score(nodes, devices, gathered, disc_weight, clean, corrupt):
    block_len = clean.shape[0]
    return pl.pallas_call(
        functools.partial(score_kernel, nodes),
        out_shape=[
            jax.ShapeDtypeStruct((2, block_len), jnp.float32),
            jax.ShapeDtypeStruct((devices, 128), jnp.float32),
        ],
        compiler_params=pltpu.CompilerParams(vmem_limit_bytes=60 * MIB),
    )(gathered, disc_weight, clean, corrupt)


def infomax(
    features,
    proj_weight,
    bias,
    disc_weight,
    adjacency,
    row_block,
    col_block,
    block_count,
    degree,
    corrupt_source,
):
    block_len = adjacency.shape[-1]
    hidden = proj_weight.shape[1]
    wide_size = lax.axis_size("wide")
    narrow_size = lax.axis_size("narrow")
    devices = wide_size * narrow_size
    wide_at = lax.axis_index("wide")
    narrow_at = lax.axis_index("narrow")
    y, zh = wide_at // ZH, wide_at % ZH
    x, zl, core = narrow_at // (ZL * CORES), narrow_at // CORES % ZL, narrow_at % CORES
    chunks = 2
    width = hidden // chunks

    own = []
    panels = []
    for h in range(chunks):
        weight = proj_weight[:, h * width : (h + 1) * width]
        part = jnp.dot(features, weight, preferred_element_type=jnp.float32)
        part = part.astype(jnp.bfloat16)
        own.append(part)
        along_z = [part]
        for k in range(1, ZH):
            along_z.append(to_wide(part, dz=k))
        along_z = jnp.stack(along_z)
        panel = [along_z]
        for k in range(1, Y):
            panel.append(to_wide(along_z, dy=k))
        panels.append(panel)

    inv_root = lax.rsqrt(degree.astype(jnp.float32))
    col_roots = lax.dynamic_index_in_dim(
        inv_root.reshape(wide_size, narrow_size, block_len), narrow_at, 1, keepdims=False
    )
    row_roots = lax.dynamic_index_in_dim(
        inv_root.reshape(wide_size, narrow_size, block_len), wide_at, 0, keepdims=False
    )
    slot_rows = row_block[0, 0]
    slot_cols = col_block[0, 0]
    slot_row_roots = row_roots[slot_rows]
    slot_col_roots = col_roots[slot_cols]
    normed = (
        adjacency[0, 0].astype(jnp.float32)
        * slot_row_roots[:, :, None]
        * slot_col_roots[:, None, :]
    ).astype(jnp.bfloat16)

    other_normed = to_narrow(normed, flip_core=1)

    slot_ids = jnp.arange(SLOTS, dtype=jnp.int32)
    columns = jnp.arange(wide_size, dtype=jnp.int32)
    sources = (
        lax.dynamic_index_in_dim(
            corrupt_source.reshape(wide_size, narrow_size), narrow_at, 1, keepdims=False
        )
        // narrow_size
    )
    tile = jnp.concatenate(
        [
            jnp.where(slot_ids < block_count[0, 0], slot_rows, narrow_size),
            slot_cols,
            jnp.sum(jnp.where(slot_cols[:, None] == columns[None, :], sources[None, :], 0), axis=1),
        ]
    )
    other = to_narrow(tile, flip_core=1)
    keys = jnp.concatenate([tile[:SLOTS], other[:SLOTS]])
    both_cols = jnp.concatenate([tile[SLOTS : 2 * SLOTS], other[SLOTS : 2 * SLOTS] + wide_size])
    both_sources = jnp.concatenate([tile[2 * SLOTS :], other[2 * SLOTS :] + wide_size])
    ids = jnp.arange(CORES * SLOTS, dtype=jnp.int32)
    before = (keys[None, :] < keys[:, None]) | (
        (keys[None, :] == keys[:, None]) & (ids[None, :] < ids[:, None])
    )
    rank = jnp.sum(before.astype(jnp.int32), axis=1)
    order = jnp.sum(jnp.where(rank[None, :] == ids[:, None], ids[None, :], 0), axis=1)
    starts = jnp.sum(
        (keys[None, :] < jnp.arange(narrow_size + 1, dtype=jnp.int32)[:, None]).astype(jnp.int32),
        axis=1,
    )
    own_source = jnp.sum(jnp.where(columns == wide_at, sources, 0))
    steps_x = jnp.arange(X, dtype=jnp.int32)
    flips = jnp.arange(ZL, dtype=jnp.int32)
    targets = ((x + steps_x)[:, None] % X * ZL + (zl ^ flips)[None, :]) * CORES + core
    dest = (y - jnp.arange(Y, dtype=jnp.int32))[:, None] % Y * ZH + (
        zh - jnp.arange(ZH, dtype=jnp.int32)
    )[None, :] % ZH
    parts = [
        order,
        both_cols,
        both_sources,
        starts,
        targets.reshape(-1),
        dest.reshape(-1),
        own_source[None],
    ]
    parts.append(jnp.zeros((META - sum(part.shape[0] for part in parts),), jnp.int32))
    meta = jnp.concatenate([part.astype(jnp.int32) for part in parts])

    groups = []
    for h in range(chunks):
        other_panel = []
        for k in range(Y):
            other_panel.append(to_narrow(panels[h][k], flip_core=1))
        split = h == chunks - 1
        *halves, own_corrupt = products(split, meta, normed, other_normed, panels[h] + other_panel)
        clean = []
        if split:
            near, far, *halves = halves
            far = to_narrow(far, flip_z=1)
        got = [halves[0]]
        for k in range(1, X):
            got.append(to_narrow(halves[k], dx=k))
        if split:
            for k in range(X):
                part = near[k].astype(jnp.float32) + far[k].astype(jnp.float32)
                part = part.astype(jnp.bfloat16)
                clean.append(to_narrow(part, dx=k) if k else part)
        far = sum(value[1].astype(jnp.float32) for value in got).astype(jnp.bfloat16)
        last = to_narrow(far, flip_z=1)
        groups.append(clean + got + [last, own[h], own_corrupt])

    own_degree = lax.dynamic_index_in_dim(
        degree.reshape(devices, block_len), wide_at * narrow_size + narrow_at, 0, keepdims=False
    )
    degree_float = own_degree.astype(jnp.float32)[:, None]
    nodes = block_len * devices
    clean_h, corrupt_h, hidden_out, spread = finish(devices, degree_float, bias[None, :], *groups)
    gathered = lax.all_to_all(spread, BOTH, 0, 0)
    scores, spread = score(nodes, devices, gathered, disc_weight, clean_h, corrupt_h)
    gathered = lax.all_to_all(spread, BOTH, 0, 0, tiled=True)
    loss = jnp.sum(gathered[:, 0]) / (2 * nodes)
    return (hidden_out, scores, loss)


def solution(mesh):
    placed = (
        P(("wide", "narrow"), None),
        P(),
        P(),
        P(),
        P("wide", "narrow", None, None, None),
        P("wide", "narrow", None),
        P("wide", "narrow", None),
        P("wide", "narrow"),
        P(),
        P(),
    )
    return jax.shard_map(
        infomax,
        mesh=mesh,
        in_specs=placed,
        out_specs=(P(("wide", "narrow"), None), P(None, ("wide", "narrow")), P()),
        check_vma=False,
    )
```
